32 devices in a mesh: groups: 2 (over y), tensor: 4 (over z), dp: 2 (over x), pipe: 2 (over core).
Axes of the slice: x: 2, y: 2, z: 4, core: 2. Of those that a mesh axis runs over, the one named last changes fastest.
Arguments:
- activations: bfloat16 [2, 2048, 8192], P('pipe', ('groups', 'dp'), 'tensor'), parts along dimension 1, may hold values from -6 to 6
- cotangents: bfloat16 [2, 2048, 8192], P('pipe', ('groups', 'dp', 'tensor')), parts along dimension 1, may hold values from -6 to 6
- out_weight: bfloat16 [2, 8192, 8192], P('pipe', 'tensor', 'dp'), may hold values from -0.0625 to 0.0625
- in_sketch: bfloat16 [2, 64, 8192], P('pipe', None, 'tensor'), may hold values from -0.25 to 0.25
- out_sketch: bfloat16 [2, 64, 8192], P('pipe'), may hold values from -0.25 to 0.25
- queries: bfloat16 [2, 512, 4096], P('pipe', 'dp', 'tensor'), may hold values from -0.09375 to 0.09375
- lengths: int32 [8], P('groups'), parts along dimension 0, may hold values from 128 to 256
- store_order: int32 [8], P('groups'), parts along dimension 0, may hold values from 0 to 3, each once
Outputs:
- act_grads: bfloat16 [2, 2048, 8192], P('pipe', ('groups', 'dp'), 'tensor'), parts along dimension 1
- sketch_store: bfloat16 [2, 8, 4096], P('pipe', ('groups', 'dp'), 'tensor'), parts along dimension 1
- scores: float32 [8, 512], P('groups', ('dp', 'tensor', 'pipe')), parts along dimension 0
The draws below stay inside these ranges and needn't reach their ends.
There are 2 independent parts, one for each index of `groups`. The reference program is written for one: setup_inputs(seed, part) draws one part's arguments, and reference() takes and returns one part's arrays. A program takes and returns all parts, laid end to end along the dimension named above; an argument that names none is the same for every part. Nothing has to cross between parts.
Inputs may be any that keep to these rules, and one draw needn't show every extreme that they name: Example e's loss covers its first lengths[e] tokens. `store_order`: a permutation of the 4 examples.
All inputs are finite; a program needn't handle non-finite values.
Results may differ from the reference program's by a relative error of at most 0.0049.
Values may be sent and summed in bfloat16 or wider, within the bound.
A program may use at most 128 MiB of HBM per device.

```python
import jax
import jax.numpy as jnp
from jax import lax

D = 8192
RANK = 64
LAY_DEV = 1
LEN = 256
TOKENS = 1024
EXAMPLES = 4
QUERIES = 512
LAYERS = 2
FEAT = 4096
N_PIPE = 2


def touch_ends(values, stream_key, smallest, largest):
    longest = values.shape.index(max(values.shape))
    spots = []
    for shift in (0, 1):
        where = [jax.random.randint(jax.random.fold_in(stream_key, axis), (), 0, length) for axis, length in enumerate(values.shape)]
        where[longest] = (where[longest] + shift) % values.shape[longest]
        spots.append(tuple(where))
    return values.at[spots[0]].set(smallest).at[spots[1]].set(largest)


def with_spikes(values, rng, source, target, shards_of, factor):
    owner, partner = [(jnp.arange(values.shape[dim]) // (values.shape[dim] // shards_of)).reshape([-1 if axis == dim else 1 for axis in range(values.ndim)]) for dim in (source, target)]
    chosen = jax.random.permutation(rng, shards_of)[partner]
    strong = (owner == chosen) | (owner == (partner + shards_of // 2) % shards_of)
    return jnp.where(strong, factor * values, values)


def block_scale(own_key, dims, split, least, largest):
    loudness = 1.0
    for dim, parts in split:
        heights = jax.random.uniform(jax.random.fold_in(jax.random.fold_in(own_key, 6), dim), (parts,), jnp.float32, least / len(split), largest / len(split))
        loudness = loudness * jnp.repeat(jnp.exp(heights), dims[dim] // parts).reshape((-1,) + (1,) * (len(dims) - 1 - dim))
    return loudness


def noise(rng, shape, spread, reach, split=(), kind=jnp.bfloat16):
    result = spread * jax.random.normal(rng, shape, jnp.float32)
    if split:
        result = result * block_scale(rng, shape, split, -0.22, 0.18)
    return jnp.clip(result, -reach, reach).astype(kind)


def heavy_noise(stream_key, dims, scale, limit, cuts, heavy, kind=jnp.bfloat16):
    array = scale * jax.random.normal(stream_key, dims, jnp.float32)
    if cuts:
        array = array * block_scale(stream_key, dims, cuts, -0.22, 0.18)
    return jnp.clip(with_spikes(array, jax.random.fold_in(stream_key, 3), *heavy), -limit, limit).astype(kind)


def setup_inputs(seed: int = 0, part: int = 0) -> dict:
    streams_of = jax.random.split(jax.random.key(seed), 9)
    own_keys = jax.random.split(jax.random.fold_in(streams_of[8], part), 9)
    activations = noise(own_keys[0], (LAYERS, TOKENS, D), 1.0, 6.0, ((0, 2), (1, 2), (2, 4)))
    cotangents = noise(own_keys[1], (LAYERS, TOKENS, D), 1.0, 6.0, ((0, 2), (1, 8)))
    out_weight = noise(streams_of[2], (LAYERS, D, D), D ** -0.5, 0.0625, ((0, 2), (1, 4), (2, 2)))
    in_sketch = noise(streams_of[3], (LAYERS, RANK, D), (D // 16) ** -0.5, 0.25, ((0, 2), (2, 4)))
    out_sketch = noise(streams_of[4], (LAYERS, RANK, D), (D // 16) ** -0.5, 0.25, ((0, 2),))
    queries = heavy_noise(streams_of[5], (LAYERS, QUERIES, FEAT), (LAYERS * FEAT) ** -0.5, 0.09375, ((0, 2), (1, 2), (2, 4)), (2, 1, 4, 2.0))
    lengths = touch_ends(jax.random.randint(own_keys[6], (EXAMPLES,), LEN // 2, LEN + 1), jax.random.fold_in(own_keys[6], 1), LEN // 2, LEN).astype(jnp.int32)
    store_order = jax.random.permutation(own_keys[7], EXAMPLES).astype(jnp.int32)
    return dict(activations=activations, cotangents=cotangents, out_weight=out_weight, in_sketch=in_sketch, out_sketch=out_sketch, queries=queries, lengths=lengths, store_order=store_order)


def reference(activations, cotangents, out_weight, in_sketch, out_sketch, queries, lengths, store_order):
    token_count = cotangents.shape[1]
    example_count = lengths.shape[0]
    token_ids = jnp.arange(token_count, dtype=jnp.int32)
    example_of = token_ids // LEN
    position = token_ids % LEN
    row_limit = jnp.take(lengths, example_of)
    loss_mask = (position < row_limit).astype(jnp.bfloat16)
    grad_list = []
    sketch_list = []
    for layer_idx in range(LAY_DEV * N_PIPE):
        masked = cotangents[layer_idx] * loss_mask[:, None]
        grad_list.append(jnp.dot(masked, out_weight[layer_idx].T, preferred_element_type=jnp.float32).astype(jnp.bfloat16))
        out_proj = jnp.dot(masked, out_sketch[layer_idx].T, preferred_element_type=jnp.float32).astype(jnp.bfloat16)
        in_proj = jnp.dot(activations[layer_idx], in_sketch[layer_idx].T, preferred_element_type=jnp.float32)
        out_rows = out_proj.astype(jnp.float32).reshape(example_count, LEN, RANK)
        in_rows = in_proj.reshape(example_count, LEN, RANK)
        outer_sum = jnp.einsum("etr,etc->erc", out_rows, in_rows, precision=lax.Precision.HIGHEST)
        outer_sum = outer_sum.reshape(example_count, RANK * RANK) / lengths.astype(jnp.float32)[:, None]
        sketch_list.append(outer_sum.astype(jnp.bfloat16))
    sketches = jnp.stack(sketch_list)
    sketch_store = jnp.take(sketches, store_order, axis=1)
    scores = jnp.einsum("lef,lqf->eq", sketches.astype(jnp.float32), queries.astype(jnp.float32), precision=lax.Precision.HIGHEST)
    return jnp.stack(grad_list), sketch_store, scores
```

```python
import functools

import jax
import jax.numpy as jnp
from jax import lax
from jax.experimental import pallas as pl
from jax.experimental.pallas import tpu as pltpu
from jax.sharding import PartitionSpec as P

MESH = pl.DeviceIdType.MESH
NT_DIMS = (((1,), (1,)), ((), ()))
F32 = jnp.float32
BF16 = jnp.bfloat16


def dot_nt(a, b):
    return lax.dot_general(a, b, NT_DIMS, preferred_element_type=F32)


def loop(lo, hi, body):
    def step(i, carry):
        body(i)
        return carry

    lax.fori_loop(lo, hi, step, 0)


def kernel(
    sizes,
    len_ref, order_ref, act_ref, cot_ref, w_ref, is_ref, os_ref, q_ref,
    grad_ref, store_ref, score_ref,
    W, G, SB, RB, ACC, O, CV, ACT, IS, OS, Q, OP, IP, SK, SR, AS, S4, ST, SP, SCR,
    zsend, zrecv, xsend, xrecv, rsend, rrecv, opsend, oprecv, sksend, skrecv,
    assend, asrecv, spsend, sprecv, loc, osem,
):
    T, D, PI, S, near, far, slab, seq = sizes
    units = near
    zi, di, pi = lax.axis_index("tensor"), lax.axis_index("dp"), lax.axis_index("pipe")
    width = W.shape[1]
    part = width // S
    feats = W.shape[0]
    half = feats // 2
    tile = min(256, half)
    E = AS.shape[2]
    RI = AS.shape[1]
    rank = IS.shape[0]
    slots = T * PI
    slot = zi * PI + pi
    up, down = zi < T - 1, zi > 0

    def cols(p):
        return pl.ds(pl.multiple_of(p * width, width), width)

    def piece(s):
        return pl.ds(s * part, part)

    def cot_piece(p, s):
        start = pl.multiple_of(p * width + s * part, part)
        return cot_ref.at[0, :, pl.ds(start, part)]

    def remote(src, dst, ss, rs, **where):
        return pltpu.make_async_remote_copy(
            src_ref=src, dst_ref=dst, send_sem=ss, recv_sem=rs, device_id=where, device_id_type=MESH
        )

    loads = [
        pltpu.make_async_copy(cot_ref.at[0], CV, loc.at[0]),
        pltpu.make_async_copy(os_ref.at[0], OS, loc.at[1]),
        pltpu.make_async_copy(w_ref.at[0], W, loc.at[2]),
        pltpu.make_async_copy(act_ref.at[0], ACT, loc.at[3]),
        pltpu.make_async_copy(is_ref.at[0], IS, loc.at[4]),
        pltpu.make_async_copy(q_ref.at[0], Q, loc.at[5]),
        pltpu.make_async_copy(cot_ref.at[0, :, cols(di)], G.at[zi, di], loc.at[6]),
    ]
    for copy in loads:
        copy.start()

    barrier = pltpu.get_barrier_semaphore()

    def greet_slot(rel):
        s = lax.rem(slot + rel, slots)
        pl.semaphore_signal(
            barrier, inc=1, device_id={"tensor": s // PI, "pipe": lax.rem(s, PI)}, device_id_type=MESH
        )

    loop(1, slots, greet_slot)
    for rel in range(1, D):
        pl.semaphore_signal(
            barrier, inc=1, device_id={"dp": lax.rem(di + rel, D)}, device_id_type=MESH
        )
    pl.semaphore_wait(barrier, slots - 1 + D - 1)

    def xcopy(p, s):
        return remote(
            cot_piece(p, s), G.at[zi, di, :, piece(s)], xsend.at[p, s], xrecv.at[di, s], dp=p
        )

    def xwait(p, s):
        remote(
            cot_piece(p, s), G.at[zi, p, :, piece(s)], xsend.at[p, s], xrecv.at[p, s], dp=p
        ).wait_recv()

    def zcopy(src, u, way, own=False):
        rel, s = units[u]
        p = lax.rem(di + rel, D)
        dst = G.at[src, p, :, piece(s)]
        source = cot_piece(di, s) if own and rel == 0 else dst
        target = zi + 1 if way == 0 else zi - 1
        return remote(source, dst, zsend.at[way, src, u], zrecv.at[src, u], tensor=target)

    def send_own(u):
        @pl.when(up)
        def _():
            zcopy(zi, u, 0, True).start()

        @pl.when(down)
        def _():
            zcopy(zi, u, 1, True).start()

    def rcopy(src, p, h):
        cut = pl.ds(h * half, half)
        return remote(
            SB.at[src, p, :, cut], RB.at[src, di, :, cut], rsend.at[src, p, h], rrecv.at[src, di, h], dp=p
        )

    def rwait(src, p):
        for h in range(2):
            cut = pl.ds(h * half, half)
            remote(
                SB.at[src, p, :, cut], RB.at[src, p, :, cut], rsend.at[src, p, h], rrecv.at[src, p, h], dp=p
            ).wait_recv()

    def opcopy(t):
        return remote(OP.at[zi], OP.at[zi], opsend.at[t], oprecv.at[zi], tensor=t)

    def skcopy(t):
        return remote(SK.at[pl.ds(t * RI, RI)], SR.at[zi], sksend.at[t], skrecv.at[zi], tensor=t)

    def ascopy(p):
        return remote(AS.at[di], AS.at[di], assend.at[p], asrecv.at[di], dp=p)

    def spcopy(s):
        return remote(
            SP.at[s], SCR.at[slot], spsend.at[s], sprecv.at[slot],
            tensor=s // PI, pipe=lax.rem(s, PI),
        )

    def others(n, me, body):
        loop(1, n, lambda rel: body(lax.rem(me + rel, n)))

    def ocopy(src):
        return pltpu.make_async_copy(
            O.at[src], grad_ref.at[pl.ds(pl.multiple_of(src * slab, slab), slab)], osem.at[src]
        )

    def row_limit(src, shape, dim):
        first = di * (T * slab) + src * slab
        return (lax.broadcasted_iota(jnp.int32, shape, dim) + lax.rem(first, seq)) < len_ref[
            first // seq
        ]

    def tiles(body, first=0, last=2):
        count = half // tile
        loop(
            first * count,
            last * count,
            lambda n: body(pl.ds(pl.multiple_of(n * tile, tile), tile)),
        )

    def partner_sums(src, p, value):
        def step(span):
            SB[src, p, :, span] = value(span).astype(BF16)

        for h in range(2):
            tiles(step, h, h + 1)
            rcopy(src, p, h).start()

    def partner_blocks(src):
        for rel in range(1, D):
            p = lax.rem(di + rel, D)
            partner_sums(src, p, lambda span, p=p: dot_nt(G[src, p], W[span, :]))

    def piece_sum(src, side, p, s, span):
        value = dot_nt(G[src, p, :, piece(s)], W[span, piece(s)])
        return value if s == 0 else ACC[side, :, span] + value

    def partner_piece(src, side, rel, s):
        p = lax.rem(di + rel, D)
        if s == S - 1:
            partner_sums(src, p, lambda span: piece_sum(src, side, p, s, span))
        else:

            def step(span):
                ACC[side, :, span] = piece_sum(src, side, p, s, span)

            tiles(step)

    def await_partners(src):
        for rel in range(1, D):
            rwait(src, lax.rem(di + rel, D))

    def with_partners(src, span, total):
        for rel in range(1, D):
            total = total + RB[src, lax.rem(di + rel, D), :, span].astype(F32)
        return total

    def finish(src, value):
        keep = row_limit(src, (slab, tile), 0)

        def step(span):
            O[src, :, span] = jnp.where(keep, value(span), 0.0).astype(BF16)

        tiles(step)
        ocopy(src).start()

    def own_block(src, side):
        def step(span):
            ACC[side, :, span] = dot_nt(G[src, di], W[span, :])

        tiles(step)
        await_partners(src)
        finish(src, lambda span: with_partners(src, span, ACC[side, :, span]))

    def own_piece(src, side, s):
        def term(span):
            value = piece_sum(src, side, di, s, span)
            return with_partners(src, span, value) if s == S - 2 else value

        if s == S - 2:
            await_partners(src)
        if s == S - 1:
            finish(src, term)
        else:

            def step(span):
                ACC[side, :, span] = term(span)

            tiles(step)

    for rel in range(1, D):
        for s in range(S):
            xcopy(lax.rem(di + rel, D), s).start()
    for u in range(S // 2):
        send_own(u)

    loads[0].wait()
    loads[1].wait()
    proj = dot_nt(OS[...], CV[...])
    OP[zi] = jnp.where(row_limit(zi, (rank, slab), 1), proj, 0.0).astype(BF16)
    others(T, zi, lambda t: opcopy(t).start())

    for u in range(S // 2, len(near)):
        rel, s = near[u]
        if rel:
            xwait(lax.rem(di + rel, D), s)
        send_own(u)

    loads[3].wait()
    loads[4].wait()
    for t in range(T):
        IP[t] = dot_nt(IS[...], ACT[t * slab : (t + 1) * slab, :])

    loads[6].wait()
    loads[2].wait()
    partner_blocks(zi)
    own_block(zi, 0)

    def op_wait(t):
        remote(OP.at[zi], OP.at[t], opsend.at[t], oprecv.at[t], tensor=t).wait_recv()

    def sketch_stage():
        others(T, zi, op_wait)
        per = T // E
        for e in range(E):
            total = jnp.zeros((rank, rank), F32)
            for t in range(e * per, (e + 1) * per):
                o, x = OP[t], IP[t]
                high = x.astype(BF16)
                rest = x - high.astype(F32)
                mid = rest.astype(BF16)
                low = (rest - mid.astype(F32)).astype(BF16)
                total = total + (dot_nt(o, high) + (dot_nt(o, mid) + dot_nt(o, low)))
            SK[:, e, :] = total
        others(T, zi, lambda t: skcopy(t).start())
        SR[zi] = SK[pl.ds(zi * RI, RI)]

    def sk_wait(t):
        remote(SK.at[pl.ds(t * RI, RI)], SR.at[t], sksend.at[t], skrecv.at[t], tensor=t).wait_recv()

    def share_stage():
        others(T, zi, sk_wait)
        total = SR[0]
        for t in range(1, T):
            total = total + SR[t]
        which = lax.broadcasted_iota(jnp.int32, total.shape, 1)
        count = jnp.zeros(total.shape, F32)
        for e in range(E):
            count = jnp.where(which == e, len_ref[di * E + e].astype(F32), count)
        AS[di] = (total / count).astype(BF16).astype(F32)
        others(D, di, lambda p: ascopy(p).start())

    def as_wait(p):
        remote(AS.at[di], AS.at[p], assend.at[p], asrecv.at[p], dp=p).wait_recv()

    def score_stage():
        others(D, di, as_wait)
        loads[5].wait()
        for p in range(D):
            for i in range(RI):
                S4[p * E : (p + 1) * E, i * rank : (i + 1) * rank] = AS[p, i]
        for r in range(E):
            wanted = order_ref[di * E + r]
            picked = jnp.zeros((1, RI * rank), F32)
            for e in range(D * E):
                picked = jnp.where(wanted == e, S4[e : e + 1, :], picked)
            ST[r : r + 1, :] = picked
        store_ref[0] = ST[...].astype(BF16)
        mine = S4[...].astype(BF16)
        share = Q.shape[0] // slots
        if share % 8 == 0:
            for s in range(slots):
                SP[s] = dot_nt(mine, Q[s * share : (s + 1) * share, :])
        else:
            total = dot_nt(mine, Q[...])
            for s in range(slots):
                SP[s] = total[:, s * share : (s + 1) * share]
        others(slots, slot, lambda s: spcopy(s).start())
        SCR[slot] = SP[slot]

    def sp_wait(s):
        remote(
            SP.at[s], SCR.at[s], spsend.at[s], sprecv.at[s], tensor=s // PI, pipe=lax.rem(s, PI)
        ).wait_recv()

    def distance(d, order):
        low, high = zi - d, zi + d

        def both(body):
            for side, (src, there) in enumerate(((low, low >= 0), (high, high < T))):

                @pl.when(there)
                def _(side=side, src=src):
                    body(src, side)

        def take(u):
            def one(src, side):
                zcopy(src, u, side).wait_recv()

                @pl.when(down if side else up)
                def _():
                    zcopy(src, u, side).start()

            both(one)

        waiting = len([u for u in order if near[u][0]])
        for count, u in enumerate(order):
            rel, s = near[u]
            take(u)
            if rel:
                waiting -= 1
                if order is far:
                    both(lambda src, side: partner_piece(src, side, rel, s))
                elif waiting == 0:
                    both(lambda src, side: partner_blocks(src))
            elif order is far:
                both(lambda src, side: own_piece(src, side, s))
            if count == 0 and order is far:

                @pl.when(d == 3)
                def _():
                    score_stage()

        if order is near_order:
            both(own_block)

    near_order = tuple(range(len(near)))
    distance(1, near_order)
    sketch_stage()

    def further(d):
        distance(d, far)

        @pl.when(d == 2)
        def _():
            share_stage()

    loop(2, T, further)

    others(slots, slot, sp_wait)
    total = SCR[0]
    for s in range(1, slots):
        total = total + SCR[s]
    score_ref[...] = total

    def drain(src):
        ocopy(src).wait()
        for rel in range(1, D):
            for h in range(2):
                rcopy(src, lax.rem(di + rel, D), h).wait_send()
        for u in range(len(units)):

            @pl.when(jnp.logical_and(up, src <= zi))
            def _(u=u):
                zcopy(src, u, 0).wait_send()

            @pl.when(jnp.logical_and(down, src >= zi))
            def _(u=u):
                zcopy(src, u, 1).wait_send()

    loop(0, T, drain)
    for rel in range(1, D):
        for s in range(S):
            xcopy(lax.rem(di + rel, D), s).wait_send()
    others(T, zi, lambda t: opcopy(t).wait_send())
    others(T, zi, lambda t: skcopy(t).wait_send())
    others(D, di, lambda p: ascopy(p).wait_send())
    others(slots, slot, lambda s: spcopy(s).wait_send())


def per_device(
    activations, cotangents, out_weight, in_sketch, out_sketch, queries, lengths, store_order
):
    T, D, PI = lax.axis_size("tensor"), lax.axis_size("dp"), lax.axis_size("pipe")
    slab, model = cotangents.shape[1:]
    feats, width = out_weight.shape[1:]
    rank = in_sketch.shape[1]
    examples = lengths.shape[0]
    E = examples // D
    RI = rank // T
    tokens = T * slab
    seq = tokens // E
    nq = queries.shape[1]
    slots = T * PI
    S = max(2, width // 1024)
    partners = [(rel, s) for rel in range(1, D) for s in range(S)]
    early = [(0, s) for s in range(S // 2)]
    near = tuple(early + partners + [(0, s) for s in range(S // 2, S)])
    far = tuple(near.index(unit) for unit in partners + [(0, s) for s in range(S)])
    NU = len(near)
    sizes = (T, D, PI, S, near, far, slab, seq)
    dma = pltpu.SemaphoreType.DMA
    smem = pl.BlockSpec(memory_space=pltpu.SMEM)
    vmem = pl.BlockSpec(memory_space=pltpu.VMEM)
    anywhere = pl.BlockSpec(memory_space=pl.ANY)
    grad, store, score = pl.pallas_call(
        functools.partial(kernel, sizes),
        out_shape=(
            jax.ShapeDtypeStruct((tokens, feats), BF16),
            jax.ShapeDtypeStruct((1, E, RI * rank), BF16),
            jax.ShapeDtypeStruct((examples, nq // slots), F32),
        ),
        in_specs=[smem, smem] + [anywhere] * 6,
        out_specs=(anywhere, vmem, vmem),
        scratch_shapes=[
            pltpu.VMEM((feats, width), BF16),
            pltpu.VMEM((T, D, slab, width), BF16),
            pltpu.VMEM((T, D, slab, feats), BF16),
            pltpu.VMEM((T, D, slab, feats), BF16),
            pltpu.VMEM((2, slab, feats), F32),
            pltpu.VMEM((T, slab, feats), BF16),
            pltpu.VMEM((slab, model), BF16),
            pltpu.VMEM(activations.shape[1:], BF16),
            pltpu.VMEM(in_sketch.shape[1:], BF16),
            pltpu.VMEM(out_sketch.shape[1:], BF16),
            pltpu.VMEM(queries.shape[1:], BF16),
            pltpu.VMEM((T, rank, slab), BF16),
            pltpu.VMEM((T, rank, slab), F32),
            pltpu.VMEM((rank, E, rank), F32),
            pltpu.VMEM((T, RI, E, rank), F32),
            pltpu.VMEM((D, RI, E, rank), F32),
            pltpu.VMEM((examples, RI * rank), F32),
            pltpu.VMEM((E, RI * rank), F32),
            pltpu.VMEM((slots, examples, nq // slots), F32),
            pltpu.VMEM((slots, examples, nq // slots), F32),
            dma((2, T, NU)), dma((T, NU)), dma((D, S)), dma((D, S)), dma((T, D, 2)), dma((T, D, 2)),
            dma((T,)), dma((T,)), dma((T,)), dma((T,)), dma((D,)), dma((D,)),
            dma((slots,)), dma((slots,)), dma((7,)), dma((T,)),
        ],
        compiler_params=pltpu.CompilerParams(collective_id=0, has_side_effects=True, vmem_limit_bytes=50 * 1024 * 1024),
        name="attribution",
    )(lengths, store_order, activations, cotangents, out_weight, in_sketch, out_sketch, queries)
    return grad[None], store, score


def solution(mesh):
    placed = (
        P("pipe", ("groups", "dp"), "tensor"),
        P("pipe", ("groups", "dp", "tensor"), None),
        P("pipe", "tensor", "dp"),
        P("pipe", None, "tensor"),
        P("pipe", None, None),
        P("pipe", "dp", "tensor"),
        P("groups"),
        P("groups"),
    )
    return jax.shard_map(
        per_device,
        mesh=mesh,
        in_specs=placed,
        out_specs=(
            P("pipe", ("groups", "dp"), "tensor"),
            P("pipe", ("groups", "dp"), "tensor"),
            P("groups", ("dp", "tensor", "pipe")),
        ),
        check_vma=False,
    )
```
